32 devices in a mesh: fsdp: 16 (over z, y, core), sp: 2 (over x).
Axes of the slice: x: 2, y: 2, z: 4, core: 2. Of those that a mesh axis runs over, the one named last changes fastest.
Arguments:
- latents: bfloat16 [32, 256, 768], P('fsdp', 'sp'), may hold values from -6 to 6
- condition: bfloat16 [32, 768], P('fsdp'), may hold values from -6 to 6
- cotangent: bfloat16 [32, 256, 768], P('fsdp', 'sp'), may hold values from -6 to 6
- w_ada: bfloat16 [768, 4608], P('fsdp'), may hold values from -0.21875 to 0.21875
- b_ada: bfloat16 [4608], P('fsdp'), may hold values from -3 to 3
- w_qkv: bfloat16 [768, 2304], P('fsdp'), may hold values from -0.21875 to 0.21875
- b_query: bfloat16 [768], P('fsdp'), may hold values from -3 to 3
- b_value: bfloat16 [768], P('fsdp'), may hold values from -3 to 3
- w_out: bfloat16 [768, 768], P('fsdp'), may hold values from -0.875 to 0.875
- b_out: bfloat16 [768], P('fsdp'), may hold values from -3 to 3
- w_up: bfloat16 [768, 3072], P('fsdp'), may hold values from -0.21875 to 0.21875
- b_up: bfloat16 [3072], P('fsdp'), may hold values from -3 to 3
- w_down: bfloat16 [3072, 768], P('fsdp'), may hold values from -0.109375 to 0.109375
- b_down: bfloat16 [768], P('fsdp'), may hold values from -3 to 3
Outputs:
- output: bfloat16 [32, 256, 768], P('fsdp', 'sp')
- grad_latents: float32 [32, 256, 768], P('fsdp', 'sp')
- grad_condition: float32 [32, 768], P('fsdp')
- grad_w_ada: float32 [768, 4608], P(('fsdp', 'sp'))
- grad_b_ada: float32 [4608], P(('fsdp', 'sp'))
- grad_w_qkv: float32 [768, 2304], P(('fsdp', 'sp'))
- grad_b_query: float32 [768], P(('fsdp', 'sp'))
- grad_b_value: float32 [768], P(('fsdp', 'sp'))
- grad_w_out: float32 [768, 768], P(('fsdp', 'sp'))
- grad_b_out: float32 [768], P(('fsdp', 'sp'))
- grad_w_up: float32 [768, 3072], P(('fsdp', 'sp'))
- grad_b_up: float32 [3072], P(('fsdp', 'sp'))
- grad_w_down: float32 [3072, 768], P(('fsdp', 'sp'))
- grad_b_down: float32 [768], P(('fsdp', 'sp'))
The draws below stay inside these ranges and needn't reach their ends.
All inputs are finite; a program needn't handle non-finite values.
Results may differ from the reference program's by a relative error of at most 0.015.
The reference program's roundings to bfloat16 on the way count: a program that leaves them out, or rounds other values in their place, can miss the bound.
Values may be sent and summed in bfloat16 or wider, within the bound.
A program may use at most 256 MiB of HBM per device.

```python
import math
import jax
import jax.numpy as jnp
from jax import lax

D = 768
H = 12
HD = 64
FF = 3072
S = 256
LATENTS = 32


def block_levels(stream_key, dims, cuts, smallest, high):
    level, own = 1.0, jax.random.fold_in(stream_key, 6)
    for position, shards_of in cuts:
        heights = jnp.exp(jax.random.uniform(jax.random.fold_in(own, position), (shards_of,), jnp.float32, smallest / len(cuts), high / len(cuts)))
        level = level * jnp.repeat(heights, dims[position] // shards_of).reshape([-1 if axis == position else 1 for axis in range(len(dims))])
    return level


def centred(stream_key, shape, spread, limit, shards=(), held_as=jnp.bfloat16):
    entries = spread * jax.random.normal(stream_key, shape, jnp.float32)
    if shards:
        entries = entries * block_levels(stream_key, shape, shards, -0.22, 0.18)
    return jnp.clip(entries, -limit, limit).astype(held_as)


def setup_inputs(seed: int = 0) -> dict:
    key_of = jax.random.split(jax.random.key(seed), 15)
    latents = centred(key_of[0], (LATENTS, S, D), 1.0, 6.0, ((0, 16), (1, 2)))
    condition = centred(key_of[1], (LATENTS, D), 1.0, 6.0, ((0, 16),))
    cotangent = centred(key_of[2], (LATENTS, S, D), 1.0, 6.0, ((0, 16), (1, 2)))
    w_ada = centred(key_of[3], (D, 6 * D), D ** -0.5, 0.21875, ((0, 16),))
    b_ada = centred(key_of[4], (6 * D,), 0.5, 3.0, ((0, 16),))
    w_qkv = centred(key_of[5], (D, 3 * D), D ** -0.5, 0.21875, ((0, 16),))
    b_query = centred(key_of[6], (D,), 0.5, 3.0, ((0, 16),))
    b_value = centred(key_of[7], (D,), 0.5, 3.0, ((0, 16),))
    w_out = centred(key_of[8], (D, D), (D // 16) ** -0.5, 0.875, ((0, 16),))
    b_out = centred(key_of[9], (D,), 0.5, 3.0, ((0, 16),))
    w_up = centred(key_of[10], (D, FF), D ** -0.5, 0.21875, ((0, 16),))
    b_up = centred(key_of[11], (FF,), 0.5, 3.0, ((0, 16),))
    w_down = centred(key_of[12], (FF, D), FF ** -0.5, 0.109375, ((0, 16),))
    b_down = centred(key_of[13], (D,), 0.5, 3.0, ((0, 16),))
    return dict(latents=latents, condition=condition, cotangent=cotangent, w_ada=w_ada, b_ada=b_ada, w_qkv=w_qkv, b_query=b_query, b_value=b_value, w_out=w_out, b_out=b_out, w_up=w_up, b_up=b_up, w_down=w_down, b_down=b_down)


eps = 1e-06

def normalize(values):
    centered = values - lax.optimization_barrier(jnp.mean(values, axis=-1, keepdims=True))
    inverse = lax.rsqrt(lax.optimization_barrier(jnp.mean(centered * centered, axis=-1, keepdims=True)) + eps)
    return (centered * inverse, inverse)

def norm_back(grad_in, normed, inverse):
    return inverse * (grad_in - lax.optimization_barrier(jnp.mean(grad_in, axis=-1, keepdims=True)) - normed * lax.optimization_barrier(jnp.mean(grad_in * normed, axis=-1, keepdims=True)))

def gelu_tanh(values):
    return jax.nn.gelu(values, approximate=True)

def silu_back(values, grad_out):
    return jax.vjp(jax.nn.silu, values)[1](grad_out)[0]

def gelu_back(values, grad_out):
    return jax.vjp(gelu_tanh, values)[1](grad_out)[0]

def group_pass(weights, group_data):
    w_ada, b_ada, w_qkv, b_query, b_value, w_out, b_out, w_up, b_up, w_down, b_down = weights
    latents, condition, cotangent = group_data
    batch_count = latents.shape[0]
    scale_factor = HD ** (-0.5)
    cond_float = condition.astype(jnp.float32)
    silu_cond = jax.nn.silu(cond_float)
    modulate = jnp.dot(silu_cond.astype(jnp.bfloat16), w_ada, preferred_element_type=jnp.float32) + b_ada.astype(jnp.float32)
    mod_parts = modulate.reshape(batch_count, 6, 1, D)
    shift_one, scale_one, gate_one = (mod_parts[:, 0], mod_parts[:, 1], mod_parts[:, 2])
    shift_two, scale_two, gate_two = (mod_parts[:, 3], mod_parts[:, 4], mod_parts[:, 5])
    inputs = latents.astype(jnp.float32)
    normed_one, inverse_one = normalize(inputs)
    attn_in = (normed_one * (1.0 + scale_one) + shift_one).astype(jnp.bfloat16)
    attn_flat = attn_in.reshape(-1, D)
    qkv_bias = jnp.concatenate([b_query, jnp.zeros_like(b_query), b_value]).astype(jnp.float32)
    projected = (jnp.dot(attn_flat, w_qkv, preferred_element_type=jnp.float32) + qkv_bias).astype(jnp.bfloat16)
    projected = projected.reshape(batch_count, S, 3, H, HD)
    queries = projected[:, :, 0].astype(jnp.float32)
    key_heads = projected[:, :, 1].astype(jnp.float32)
    value_heads = projected[:, :, 2].astype(jnp.float32)
    scores = jnp.einsum('bqhd,bkhd->bhqk', queries, key_heads) * scale_factor
    log_total = jnp.log(lax.optimization_barrier(jnp.sum(jnp.exp(scores), axis=-1, keepdims=True)))
    soft_float = jnp.exp(scores - log_total)
    soft_half = soft_float.astype(jnp.bfloat16)
    mixed = jnp.einsum('bhqk,bkhd->bqhd', soft_half.astype(jnp.float32), value_heads).astype(jnp.bfloat16)
    mixed_flat = mixed.reshape(-1, D)
    attn_proj = (jnp.dot(mixed_flat, w_out, preferred_element_type=jnp.float32) + b_out.astype(jnp.float32)).reshape(batch_count, S, D)
    residual = inputs + gate_one * attn_proj
    normed_two, inverse_two = normalize(residual)
    mlp_in = (normed_two * (1.0 + scale_two) + shift_two).astype(jnp.bfloat16).reshape(-1, D)
    up_value = jnp.dot(mlp_in, w_up, preferred_element_type=jnp.float32) + b_up.astype(jnp.float32)
    activated = gelu_tanh(up_value).astype(jnp.bfloat16)
    down_value = (jnp.dot(activated, w_down, preferred_element_type=jnp.float32) + b_down.astype(jnp.float32)).reshape(batch_count, S, D)
    output = (residual + gate_two * down_value).astype(jnp.bfloat16)
    grad_out = cotangent.astype(jnp.float32)
    grad_gate_two = lax.optimization_barrier(jnp.sum(grad_out * down_value, axis=1))
    grad_down = (grad_out * gate_two).astype(jnp.bfloat16).reshape(-1, D)
    gw_down = jnp.dot(activated.T, grad_down, preferred_element_type=jnp.float32)
    gb_down = lax.optimization_barrier(jnp.sum(grad_down.astype(jnp.float32), axis=0))
    grad_act = jnp.dot(grad_down, w_down.T, preferred_element_type=jnp.float32)
    grad_up = gelu_back(up_value, grad_act).astype(jnp.bfloat16)
    gw_up = jnp.dot(mlp_in.T, grad_up, preferred_element_type=jnp.float32)
    gb_up = lax.optimization_barrier(jnp.sum(grad_up.astype(jnp.float32), axis=0))
    grad_mlp = jnp.dot(grad_up, w_up.T, preferred_element_type=jnp.float32).reshape(batch_count, S, D)
    grad_scale_two = lax.optimization_barrier(jnp.sum(grad_mlp * normed_two, axis=1))
    grad_shift_two = lax.optimization_barrier(jnp.sum(grad_mlp, axis=1))
    grad_resid = grad_out + norm_back(grad_mlp * (1.0 + scale_two), normed_two, inverse_two)
    grad_gate_one = lax.optimization_barrier(jnp.sum(grad_resid * attn_proj, axis=1))
    grad_proj = (grad_resid * gate_one).astype(jnp.bfloat16).reshape(-1, D)
    gw_out = jnp.dot(mixed_flat.T, grad_proj, preferred_element_type=jnp.float32)
    gb_out = lax.optimization_barrier(jnp.sum(grad_proj.astype(jnp.float32), axis=0))
    grad_mixed = jnp.dot(grad_proj, w_out.T, preferred_element_type=jnp.float32).astype(jnp.bfloat16)
    grad_mixed = grad_mixed.reshape(batch_count, S, H, HD).astype(jnp.float32)
    grad_soft = jnp.einsum('bqhd,bkhd->bhqk', grad_mixed, value_heads)
    delta_sum = lax.optimization_barrier(jnp.sum(soft_float * grad_soft, axis=-1, keepdims=True))
    grad_scores = (soft_float * (grad_soft - delta_sum)).astype(jnp.bfloat16).astype(jnp.float32)
    grad_queries = (jnp.einsum('bhqk,bkhd->bqhd', grad_scores, key_heads) * scale_factor).astype(jnp.bfloat16)
    grad_keys = (jnp.einsum('bhqk,bqhd->bkhd', grad_scores, queries) * scale_factor).astype(jnp.bfloat16)
    grad_values = jnp.einsum('bhqk,bqhd->bkhd', soft_half.astype(jnp.float32), grad_mixed).astype(jnp.bfloat16)
    grad_qkv = jnp.stack([grad_queries, grad_keys, grad_values], axis=2).reshape(-1, 3 * D)
    gw_qkv = jnp.dot(attn_flat.T, grad_qkv, preferred_element_type=jnp.float32)
    gb_query = lax.optimization_barrier(jnp.sum(grad_queries.astype(jnp.float32), axis=(0, 1))).reshape(D)
    gb_value = lax.optimization_barrier(jnp.sum(grad_values.astype(jnp.float32), axis=(0, 1))).reshape(D)
    grad_attn_in = jnp.dot(grad_qkv, w_qkv.T, preferred_element_type=jnp.float32).reshape(batch_count, S, D)
    grad_scale_one = lax.optimization_barrier(jnp.sum(grad_attn_in * normed_one, axis=1))
    grad_shift_one = lax.optimization_barrier(jnp.sum(grad_attn_in, axis=1))
    grad_latents = grad_resid + norm_back(grad_attn_in * (1.0 + scale_one), normed_one, inverse_one)
    grad_mod = jnp.concatenate([grad_shift_one, grad_scale_one, grad_gate_one, grad_shift_two, grad_scale_two, grad_gate_two], axis=1)
    gw_ada = jnp.dot(silu_cond.T, grad_mod, precision=lax.Precision.HIGHEST)
    gb_ada = lax.optimization_barrier(jnp.sum(grad_mod, axis=0))
    grad_silu = jnp.dot(grad_mod.astype(jnp.bfloat16), w_ada.T, preferred_element_type=jnp.float32)
    grad_condition = silu_back(cond_float, grad_silu)
    grads = (gw_ada, gb_ada, gw_qkv, gb_query, gb_value, gw_out, gb_out, gw_up, gb_up, gw_down, gb_down)
    return ((output, grad_latents, grad_condition), grads)

def reference(latents, condition, cotangent, w_ada, b_ada, w_qkv, b_query, b_value, w_out, b_out, w_up, b_up, w_down, b_down):
    weights = (w_ada, b_ada, w_qkv, b_query, b_value, w_out, b_out, w_up, b_up, w_down, b_down)
    latent_total = latents.shape[0]
    group_size = math.gcd(latent_total, 16)
    group_count = latent_total // group_size
    stacked = (latents.reshape(group_count, group_size, S, D), condition.reshape(group_count, group_size, D), cotangent.reshape(group_count, group_size, S, D))

    def scan_step(running, group_data):
        outcome, grads = group_pass(weights, group_data)
        return (jax.tree.map(jnp.add, running, grads), outcome)
    zero_grads = tuple((jnp.zeros(weight.shape, jnp.float32) for weight in weights))
    grads, outcome = lax.scan(scan_step, zero_grads, stacked)
    output = outcome[0].reshape(latent_total, S, D)
    grad_latents = outcome[1].reshape(latent_total, S, D)
    grad_condition = outcome[2].reshape(latent_total, D)
    return (output, grad_latents, grad_condition, grads[0], grads[1], grads[2], grads[3], grads[4], grads[5], grads[6], grads[7], grads[8], grads[9], grads[10])
```

```python
import jax
import jax.numpy as jnp
from jax import lax
from jax.sharding import PartitionSpec as P

D = 768
H = 12
HD = 64


eps = 1e-06


def normalize(values):
    centered = values - jnp.mean(values, axis=-1, keepdims=True)
    inverse = lax.rsqrt(jnp.mean(centered * centered, axis=-1, keepdims=True) + eps)
    return (centered * inverse, inverse)


def norm_back(grad_in, normed, inverse):
    return inverse * (
        grad_in
        - jnp.mean(grad_in, axis=-1, keepdims=True)
        - normed * jnp.mean(grad_in * normed, axis=-1, keepdims=True)
    )


def gelu_tanh(values):
    return jax.nn.gelu(values, approximate=True)


def silu_back(values, grad_out):
    return jax.vjp(jax.nn.silu, values)[1](grad_out)[0]


def gelu_back(values, grad_out):
    return jax.vjp(gelu_tanh, values)[1](grad_out)[0]


LANES = 2048


def reduce_rows(grad):
    return lax.psum_scatter(
        grad.astype(jnp.bfloat16), ("fsdp", "sp"), scatter_dimension=0, tiled=True
    ).astype(jnp.float32)


def body(
    latents,
    condition,
    cotangent,
    w_ada,
    b_ada,
    w_qkv,
    b_query,
    b_value,
    w_out,
    b_out,
    w_up,
    b_up,
    w_down,
    b_down,
):
    f32 = jnp.float32
    bf16 = jnp.bfloat16
    fsdp_count = lax.axis_size("fsdp")
    sp_count = lax.axis_size("sp")
    owners = fsdp_count * sp_count
    fsdp_index = lax.axis_index("fsdp")
    sp_index = lax.axis_index("sp")
    owner_index = fsdp_index * sp_count + sp_index
    pair_latents = latents.shape[0]
    own_latents = pair_latents // sp_count
    latent_total = pair_latents * fsdp_count
    tokens_all = latents.shape[1] * sp_count
    scale_factor = HD ** (-0.5)

    small = [condition.reshape(-1), b_ada, b_query, b_value, b_out, b_up, b_down]
    width = sum(part.size for part in small)
    padded = -(-width // LANES) * LANES
    small.append(jnp.zeros((padded - width,), bf16))
    small_all = lax.all_gather(
        jnp.concatenate(small).reshape(1, padded // 128, 128), "fsdp", axis=0, tiled=True
    ).reshape(fsdp_count, padded)
    pieces = []
    start = 0
    for part in small[:-1]:
        pieces.append(small_all[:, start : start + part.size].reshape(-1))
        start = start + part.size
    cond_all, ada_bias, query_bias, value_bias, out_bias, up_bias, down_bias = pieces
    cond_all = cond_all.reshape(latent_total, D).astype(f32)
    silu_all = jax.nn.silu(cond_all)

    inputs = lax.all_to_all(latents, "sp", split_axis=0, concat_axis=1, tiled=True).astype(f32)
    grad_out = lax.all_to_all(cotangent, "sp", split_axis=0, concat_axis=1, tiled=True).astype(f32)

    ada_rows = w_ada.shape[0]
    silu_mine = lax.dynamic_index_in_dim(
        silu_all.astype(bf16).reshape(fsdp_count, sp_count, own_latents, D), sp_index, 1, False
    )
    silu_mine = lax.dynamic_index_in_dim(
        silu_mine.reshape(fsdp_count * own_latents, fsdp_count, ada_rows), fsdp_index, 1, False
    )
    mod_part = jnp.dot(silu_mine, w_ada, preferred_element_type=f32)
    mod_part = lax.all_to_all(
        mod_part.reshape(fsdp_count, own_latents * 6 * D), "fsdp", split_axis=0, concat_axis=0, tiled=True
    )
    modulate = jnp.sum(mod_part, axis=0).reshape(own_latents, 6 * D) + ada_bias.astype(f32)
    mod_parts = modulate.reshape(own_latents, 6, 1, D)
    shift_one, scale_one, gate_one = (mod_parts[:, 0], mod_parts[:, 1], mod_parts[:, 2])
    shift_two, scale_two, gate_two = (mod_parts[:, 3], mod_parts[:, 4], mod_parts[:, 5])

    qkv_full = lax.all_gather(w_qkv, "fsdp", axis=0, tiled=True)
    out_full = lax.all_gather(w_out, "fsdp", axis=0, tiled=True)
    up_full = lax.all_gather(w_up, "fsdp", axis=0, tiled=True)
    down_full = lax.all_gather(w_down, "fsdp", axis=0, tiled=True)

    normed_one, inverse_one = normalize(inputs)
    attn_in = (normed_one * (1.0 + scale_one) + shift_one).astype(bf16)
    qkv_bias = jnp.concatenate([query_bias, jnp.zeros_like(query_bias), value_bias]).astype(f32)
    projected = (
        jnp.einsum("btd,de->bte", attn_in, qkv_full, preferred_element_type=f32) + qkv_bias
    ).astype(bf16)
    heads = projected.reshape(own_latents, tokens_all, 3, H, HD).transpose(2, 0, 3, 1, 4)
    queries, key_heads, value_heads = heads[0], heads[1], heads[2]
    scores = (
        jnp.einsum("bhqd,bhkd->bhqk", queries, key_heads, preferred_element_type=f32) * scale_factor
    )
    log_total = jnp.log(jnp.sum(jnp.exp(scores), axis=-1, keepdims=True))
    soft_float = jnp.exp(scores - log_total)
    soft_half = soft_float.astype(bf16)
    mixed = jnp.einsum("bhqk,bhkd->bhqd", soft_half, value_heads, preferred_element_type=f32).astype(
        bf16
    )
    mixed_tokens = mixed.transpose(0, 2, 1, 3).reshape(own_latents, tokens_all, D)
    attn_proj = jnp.einsum(
        "btd,de->bte", mixed_tokens, out_full, preferred_element_type=f32
    ) + out_bias.astype(f32)
    residual = inputs + gate_one * attn_proj
    normed_two, inverse_two = normalize(residual)
    mlp_in = (normed_two * (1.0 + scale_two) + shift_two).astype(bf16)
    up_value = jnp.einsum(
        "btd,df->btf", mlp_in, up_full, preferred_element_type=f32
    ) + up_bias.astype(f32)
    activated = gelu_tanh(up_value).astype(bf16)
    down_value = jnp.einsum(
        "btf,fd->btd", activated, down_full, preferred_element_type=f32
    ) + down_bias.astype(f32)
    output = (residual + gate_two * down_value).astype(bf16)
    output = lax.all_to_all(output, "sp", split_axis=1, concat_axis=0, tiled=True)

    grad_gate_two = jnp.sum(grad_out * down_value, axis=1)
    grad_down = (grad_out * gate_two).astype(bf16)
    gw_down = jnp.einsum("btf,btd->fd", activated, grad_down, preferred_element_type=f32)
    own_down = reduce_rows(gw_down)
    gb_down = jnp.sum(grad_down.astype(f32), axis=(0, 1))
    grad_act = jnp.einsum("btd,fd->btf", grad_down, down_full, preferred_element_type=f32)
    grad_up = gelu_back(up_value, grad_act).astype(bf16)
    gw_up = jnp.einsum("btd,btf->df", mlp_in, grad_up, preferred_element_type=f32)
    own_up = reduce_rows(gw_up)
    gb_up = jnp.sum(grad_up.astype(f32), axis=(0, 1))
    grad_mlp = jnp.einsum("btf,df->btd", grad_up, up_full, preferred_element_type=f32)
    grad_scale_two = jnp.sum(grad_mlp * normed_two, axis=1)
    grad_shift_two = jnp.sum(grad_mlp, axis=1)
    grad_resid = grad_out + norm_back(grad_mlp * (1.0 + scale_two), normed_two, inverse_two)
    grad_gate_one = jnp.sum(grad_resid * attn_proj, axis=1)
    grad_proj = (grad_resid * gate_one).astype(bf16)
    gw_out = jnp.einsum("btd,bte->de", mixed_tokens, grad_proj, preferred_element_type=f32)
    own_out = reduce_rows(gw_out)
    gb_out = jnp.sum(grad_proj.astype(f32), axis=(0, 1))
    grad_mixed = jnp.einsum("bte,de->btd", grad_proj, out_full, preferred_element_type=f32).astype(
        bf16
    )
    grad_heads = grad_mixed.reshape(own_latents, tokens_all, H, HD).transpose(0, 2, 1, 3)
    grad_soft = jnp.einsum("bhqd,bhkd->bhqk", grad_heads, value_heads, preferred_element_type=f32)
    delta_sum = jnp.sum(soft_float * grad_soft, axis=-1, keepdims=True)
    grad_scores = (soft_float * (grad_soft - delta_sum)).astype(bf16)
    grad_queries = (
        jnp.einsum("bhqk,bhkd->bhqd", grad_scores, key_heads, preferred_element_type=f32)
        * scale_factor
    ).astype(bf16)
    grad_keys = (
        jnp.einsum("bhqk,bhqd->bhkd", grad_scores, queries, preferred_element_type=f32)
        * scale_factor
    ).astype(bf16)
    grad_values = jnp.einsum(
        "bhqk,bhqd->bhkd", soft_half, grad_heads, preferred_element_type=f32
    ).astype(bf16)
    grad_tokens = (
        jnp.stack([grad_queries, grad_keys, grad_values], axis=0)
        .transpose(1, 3, 0, 2, 4)
        .reshape(own_latents, tokens_all, 3 * D)
    )
    gw_qkv = jnp.einsum("btd,bte->de", attn_in, grad_tokens, preferred_element_type=f32)
    own_qkv = reduce_rows(gw_qkv)
    grad_tok_float = grad_tokens.astype(f32)
    gb_query = jnp.sum(grad_tok_float[:, :, :D], axis=(0, 1))
    gb_value = jnp.sum(grad_tok_float[:, :, 2 * D :], axis=(0, 1))
    grad_attn_in = jnp.einsum("bte,de->btd", grad_tokens, qkv_full, preferred_element_type=f32)
    grad_scale_one = jnp.sum(grad_attn_in * normed_one, axis=1)
    grad_shift_one = jnp.sum(grad_attn_in, axis=1)
    grad_latents = grad_resid + norm_back(grad_attn_in * (1.0 + scale_one), normed_one, inverse_one)
    grad_latents = lax.all_to_all(grad_latents, "sp", split_axis=1, concat_axis=0, tiled=True)

    grad_small = [
        grad_shift_one.reshape(-1),
        grad_scale_one.reshape(-1),
        grad_gate_one.reshape(-1),
        grad_shift_two.reshape(-1),
        grad_scale_two.reshape(-1),
        grad_gate_two.reshape(-1),
        gb_query,
        gb_value,
        gb_out,
        gb_up,
        gb_down,
    ]
    grad_small_all = lax.all_gather(jnp.concatenate(grad_small), ("fsdp", "sp"), axis=0)
    mod_width = 6 * own_latents * D
    grad_mod = (
        grad_small_all[:, :mod_width]
        .reshape(owners, 6, own_latents, D)
        .transpose(0, 2, 1, 3)
        .reshape(latent_total, 6 * D)
    )
    bias_sums = jnp.sum(grad_small_all[:, mod_width:], axis=0)
    own_bias = []
    start = 0
    for part in grad_small[6:]:
        piece = bias_sums[start : start + part.size].reshape(owners, -1)
        own_bias.append(lax.dynamic_index_in_dim(piece, owner_index, 0, False))
        start = start + part.size
    own_gb_query, own_gb_value, own_gb_out, own_gb_up, own_gb_down = own_bias
    silu_rows = lax.dynamic_index_in_dim(
        silu_all.reshape(latent_total, owners, D // owners), owner_index, 1, False
    )
    own_ada = jnp.dot(silu_rows.T, grad_mod, precision=lax.Precision.HIGHEST)
    own_gb_ada = lax.dynamic_index_in_dim(
        jnp.sum(grad_mod, axis=0).reshape(owners, -1), owner_index, 0, False
    )
    grad_silu = jnp.dot(grad_mod.astype(bf16), w_ada.T, preferred_element_type=f32)
    grad_silu = lax.all_to_all(
        grad_silu.reshape(fsdp_count, pair_latents * ada_rows),
        "fsdp",
        split_axis=0,
        concat_axis=0,
        tiled=True,
    )
    grad_silu = (
        grad_silu.reshape(fsdp_count, pair_latents, ada_rows)
        .transpose(1, 0, 2)
        .reshape(pair_latents, D)
    )
    grad_condition = silu_back(condition.astype(f32), grad_silu)
    return (
        output,
        grad_latents,
        grad_condition,
        own_ada,
        own_gb_ada,
        own_qkv,
        own_gb_query,
        own_gb_value,
        own_out,
        own_gb_out,
        own_up,
        own_gb_up,
        own_down,
        own_gb_down,
    )


def solution(mesh):
    in_specs = (
        P("fsdp", "sp", None),
        P("fsdp", None),
        P("fsdp", "sp", None),
        P("fsdp", None),
        P("fsdp"),
        P("fsdp", None),
        P("fsdp"),
        P("fsdp"),
        P("fsdp", None),
        P("fsdp"),
        P("fsdp", None),
        P("fsdp"),
        P("fsdp", None),
        P("fsdp"),
    )
    out_specs = (
        P("fsdp", "sp", None),
        P("fsdp", "sp", None),
        P("fsdp", None),
        P(("fsdp", "sp"), None),
        P(("fsdp", "sp")),
        P(("fsdp", "sp"), None),
        P(("fsdp", "sp")),
        P(("fsdp", "sp")),
        P(("fsdp", "sp"), None),
        P(("fsdp", "sp")),
        P(("fsdp", "sp"), None),
        P(("fsdp", "sp")),
        P(("fsdp", "sp"), None),
        P(("fsdp", "sp")),
    )
    return jax.shard_map(body, mesh=mesh, in_specs=in_specs, out_specs=out_specs, check_vma=False)
```

```python
import jax
import jax.numpy as jnp
from jax import lax
from jax.sharding import PartitionSpec as P

D = 768
H = 12
HD = 64


eps = 1e-06


def normalize(values):
    centered = values - jnp.mean(values, axis=-1, keepdims=True)
    inverse = lax.rsqrt(jnp.mean(centered * centered, axis=-1, keepdims=True) + eps)
    return (centered * inverse, inverse)


def norm_back(grad_in, normed, inverse):
    return inverse * (
        grad_in
        - jnp.mean(grad_in, axis=-1, keepdims=True)
        - normed * jnp.mean(grad_in * normed, axis=-1, keepdims=True)
    )


def gelu_tanh(values):
    return jax.nn.gelu(values, approximate=True)


def silu_back(values, grad_out):
    return jax.vjp(jax.nn.silu, values)[1](grad_out)[0]


def gelu_back(values, grad_out):
    return jax.vjp(gelu_tanh, values)[1](grad_out)[0]


LANES = 2048


def body(
    latents,
    condition,
    cotangent,
    w_ada,
    b_ada,
    w_qkv,
    b_query,
    b_value,
    w_out,
    b_out,
    w_up,
    b_up,
    w_down,
    b_down,
):
    f32 = jnp.float32
    bf16 = jnp.bfloat16
    fsdp_count = lax.axis_size("fsdp")
    sp_count = lax.axis_size("sp")
    owners = fsdp_count * sp_count
    fsdp_index = lax.axis_index("fsdp")
    sp_index = lax.axis_index("sp")
    owner_index = fsdp_index * sp_count + sp_index
    pair_latents = latents.shape[0]
    own_latents = pair_latents // sp_count
    latent_total = pair_latents * fsdp_count
    tokens_all = latents.shape[1] * sp_count
    scale_factor = HD ** (-0.5)

    small = [condition.reshape(-1), b_ada, b_query, b_value, b_out, b_up, b_down]
    width = sum(part.size for part in small)
    padded = -(-width // LANES) * LANES
    small.append(jnp.zeros((padded - width,), bf16))
    small_all = lax.all_gather(
        jnp.concatenate(small).reshape(1, padded // 128, 128), "fsdp", axis=0, tiled=True
    ).reshape(fsdp_count, padded)
    pieces = []
    start = 0
    for part in small[:-1]:
        pieces.append(small_all[:, start : start + part.size].reshape(-1))
        start = start + part.size
    cond_all, ada_bias, query_bias, value_bias, out_bias, up_bias, down_bias = pieces
    cond_all = cond_all.reshape(latent_total, D).astype(f32)
    silu_all = jax.nn.silu(cond_all)

    inputs = lax.all_to_all(latents, "sp", split_axis=0, concat_axis=1, tiled=True).astype(f32)
    grad_out = lax.all_to_all(cotangent, "sp", split_axis=0, concat_axis=1, tiled=True).astype(f32)

    ada_rows = w_ada.shape[0]
    silu_mine = lax.dynamic_index_in_dim(
        silu_all.astype(bf16).reshape(fsdp_count, sp_count, own_latents, D), sp_index, 1, False
    )
    silu_mine = lax.dynamic_index_in_dim(
        silu_mine.reshape(fsdp_count * own_latents, fsdp_count, ada_rows), fsdp_index, 1, False
    )
    mod_part = jnp.dot(silu_mine, w_ada, preferred_element_type=f32)
    mod_part = lax.all_to_all(
        mod_part.reshape(fsdp_count, own_latents * 6 * D), "fsdp", split_axis=0, concat_axis=0, tiled=True
    )
    modulate = jnp.sum(mod_part, axis=0).reshape(own_latents, 6 * D) + ada_bias.astype(f32)
    mod_parts = modulate.reshape(own_latents, 6, 1, D)
    shift_one, scale_one, gate_one = (mod_parts[:, 0], mod_parts[:, 1], mod_parts[:, 2])
    shift_two, scale_two, gate_two = (mod_parts[:, 3], mod_parts[:, 4], mod_parts[:, 5])

    qkv_full = lax.all_gather(w_qkv, "fsdp", axis=0, tiled=True)
    out_full = lax.all_gather(w_out, "fsdp", axis=0, tiled=True)
    up_full = lax.all_gather(w_up, "fsdp", axis=0, tiled=True)
    down_full = lax.all_gather(w_down, "fsdp", axis=0, tiled=True)

    normed_one, inverse_one = normalize(inputs)
    attn_in = (normed_one * (1.0 + scale_one) + shift_one).astype(bf16)
    qkv_bias = jnp.concatenate([query_bias, jnp.zeros_like(query_bias), value_bias]).astype(f32)
    projected = (
        jnp.einsum("btd,de->bte", attn_in, qkv_full, preferred_element_type=f32) + qkv_bias
    ).astype(bf16)
    heads = projected.reshape(own_latents, tokens_all, 3, H, HD).transpose(2, 0, 3, 1, 4)
    queries, key_heads, value_heads = heads[0], heads[1], heads[2]
    scores = (
        jnp.einsum("bhqd,bhkd->bhqk", queries, key_heads, preferred_element_type=f32) * scale_factor
    )
    log_total = jnp.log(jnp.sum(jnp.exp(scores), axis=-1, keepdims=True))
    soft_float = jnp.exp(scores - log_total)
    soft_half = soft_float.astype(bf16)
    mixed = jnp.einsum("bhqk,bhkd->bhqd", soft_half, value_heads, preferred_element_type=f32).astype(
        bf16
    )
    mixed_tokens = mixed.transpose(0, 2, 1, 3).reshape(own_latents, tokens_all, D)
    attn_proj = jnp.einsum(
        "btd,de->bte", mixed_tokens, out_full, preferred_element_type=f32
    ) + out_bias.astype(f32)
    residual = inputs + gate_one * attn_proj
    normed_two, inverse_two = normalize(residual)
    mlp_in = (normed_two * (1.0 + scale_two) + shift_two).astype(bf16)
    up_value = jnp.einsum(
        "btd,df->btf", mlp_in, up_full, preferred_element_type=f32
    ) + up_bias.astype(f32)
    activated = gelu_tanh(up_value).astype(bf16)
    down_value = jnp.einsum(
        "btf,fd->btd", activated, down_full, preferred_element_type=f32
    ) + down_bias.astype(f32)
    output = (residual + gate_two * down_value).astype(bf16)
    output = lax.all_to_all(output, "sp", split_axis=1, concat_axis=0, tiled=True)

    grad_gate_two = jnp.sum(grad_out * down_value, axis=1)
    grad_down = (grad_out * gate_two).astype(bf16)
    gw_down = jnp.einsum("btf,btd->fd", activated, grad_down, preferred_element_type=f32)
    gb_down = jnp.sum(grad_down.astype(f32), axis=(0, 1))
    grad_act = jnp.einsum("btd,fd->btf", grad_down, down_full, preferred_element_type=f32)
    grad_up = gelu_back(up_value, grad_act).astype(bf16)
    gw_up = jnp.einsum("btd,btf->df", mlp_in, grad_up, preferred_element_type=f32)
    gb_up = jnp.sum(grad_up.astype(f32), axis=(0, 1))
    grad_mlp = jnp.einsum("btf,df->btd", grad_up, up_full, preferred_element_type=f32)
    grad_scale_two = jnp.sum(grad_mlp * normed_two, axis=1)
    grad_shift_two = jnp.sum(grad_mlp, axis=1)
    grad_resid = grad_out + norm_back(grad_mlp * (1.0 + scale_two), normed_two, inverse_two)
    grad_gate_one = jnp.sum(grad_resid * attn_proj, axis=1)
    grad_proj = (grad_resid * gate_one).astype(bf16)
    gw_out = jnp.einsum("btd,bte->de", mixed_tokens, grad_proj, preferred_element_type=f32)
    gb_out = jnp.sum(grad_proj.astype(f32), axis=(0, 1))
    grad_mixed = jnp.einsum("bte,de->btd", grad_proj, out_full, preferred_element_type=f32).astype(
        bf16
    )
    grad_heads = grad_mixed.reshape(own_latents, tokens_all, H, HD).transpose(0, 2, 1, 3)
    grad_soft = jnp.einsum("bhqd,bhkd->bhqk", grad_heads, value_heads, preferred_element_type=f32)
    delta_sum = jnp.sum(soft_float * grad_soft, axis=-1, keepdims=True)
    grad_scores = (soft_float * (grad_soft - delta_sum)).astype(bf16)
    grad_queries = (
        jnp.einsum("bhqk,bhkd->bhqd", grad_scores, key_heads, preferred_element_type=f32)
        * scale_factor
    ).astype(bf16)
    grad_keys = (
        jnp.einsum("bhqk,bhqd->bhkd", grad_scores, queries, preferred_element_type=f32)
        * scale_factor
    ).astype(bf16)
    grad_values = jnp.einsum(
        "bhqk,bhqd->bhkd", soft_half, grad_heads, preferred_element_type=f32
    ).astype(bf16)
    grad_tokens = (
        jnp.stack([grad_queries, grad_keys, grad_values], axis=0)
        .transpose(1, 3, 0, 2, 4)
        .reshape(own_latents, tokens_all, 3 * D)
    )
    gw_qkv = jnp.einsum("btd,bte->de", attn_in, grad_tokens, preferred_element_type=f32)
    grad_tok_float = grad_tokens.astype(f32)
    gb_query = jnp.sum(grad_tok_float[:, :, :D], axis=(0, 1))
    gb_value = jnp.sum(grad_tok_float[:, :, 2 * D :], axis=(0, 1))
    grad_attn_in = jnp.einsum("bte,de->btd", grad_tokens, qkv_full, preferred_element_type=f32)
    grad_scale_one = jnp.sum(grad_attn_in * normed_one, axis=1)
    grad_shift_one = jnp.sum(grad_attn_in, axis=1)
    grad_latents = grad_resid + norm_back(grad_attn_in * (1.0 + scale_one), normed_one, inverse_one)
    grad_latents = lax.all_to_all(grad_latents, "sp", split_axis=1, concat_axis=0, tiled=True)

    grad_mod = jnp.concatenate(
        [
            grad_shift_one,
            grad_scale_one,
            grad_gate_one,
            grad_shift_two,
            grad_scale_two,
            grad_gate_two,
        ],
        axis=1,
    )
    grad_mod = lax.all_to_all(
        jnp.broadcast_to(grad_mod[None], (owners, own_latents, 6 * D)),
        ("fsdp", "sp"),
        split_axis=0,
        concat_axis=0,
        tiled=True,
    ).reshape(latent_total, 6 * D)

    rows = D // owners
    biases = (gb_query, gb_value, gb_out, gb_up, gb_down)
    bias_rows = jnp.concatenate([part.reshape(owners, -1) for part in biases], axis=1)
    bias_width = bias_rows.shape[1]
    bias_lanes = -(-bias_width // (rows * 128)) * 128
    bias_rows = jnp.pad(bias_rows, ((0, 0), (0, rows * bias_lanes - bias_width)))
    stack = down_full.shape[0] // D
    gw_down = (
        gw_down.astype(bf16)
        .reshape(owners, stack, rows, D)
        .transpose(0, 2, 1, 3)
        .reshape(D, stack * D)
    )
    packed = jnp.concatenate(
        [
            gw_down,
            gw_up.astype(bf16),
            gw_qkv.astype(bf16),
            gw_out.astype(bf16),
            bias_rows.astype(bf16).reshape(D, bias_lanes),
        ],
        axis=1,
    )
    owned = lax.psum_scatter(packed, ("fsdp", "sp"), scatter_dimension=0, tiled=True).astype(f32)
    own_weights = []
    start = 0
    for width in (stack * D, up_full.shape[1], 3 * D, D, bias_lanes):
        own_weights.append(owned[:, start : start + width])
        start = start + width
    own_down, own_up, own_qkv, own_out, bias_sums = own_weights
    own_down = own_down.reshape(rows, stack, D).transpose(1, 0, 2).reshape(stack * rows, D)
    bias_sums = bias_sums.reshape(-1)
    own_bias = []
    start = 0
    for part in biases:
        width = part.size // owners
        own_bias.append(bias_sums[start : start + width])
        start = start + width
    own_gb_query, own_gb_value, own_gb_out, own_gb_up, own_gb_down = own_bias
    silu_rows = lax.dynamic_index_in_dim(
        silu_all.reshape(latent_total, owners, D // owners), owner_index, 1, False
    )
    own_ada = jnp.dot(silu_rows.T, grad_mod, precision=lax.Precision.HIGHEST)
    own_gb_ada = lax.dynamic_index_in_dim(
        jnp.sum(grad_mod, axis=0).reshape(owners, -1), owner_index, 0, False
    )
    grad_silu = jnp.dot(grad_mod.astype(bf16), w_ada.T, preferred_element_type=f32)
    grad_silu = lax.all_to_all(
        grad_silu.reshape(fsdp_count, pair_latents * ada_rows),
        "fsdp",
        split_axis=0,
        concat_axis=0,
        tiled=True,
    )
    grad_silu = (
        grad_silu.reshape(fsdp_count, pair_latents, ada_rows)
        .transpose(1, 0, 2)
        .reshape(pair_latents, D)
    )
    grad_condition = silu_back(condition.astype(f32), grad_silu)
    return (
        output,
        grad_latents,
        grad_condition,
        own_ada,
        own_gb_ada,
        own_qkv,
        own_gb_query,
        own_gb_value,
        own_out,
        own_gb_out,
        own_up,
        own_gb_up,
        own_down,
        own_gb_down,
    )


def solution(mesh):
    in_specs = (
        P("fsdp", "sp", None),
        P("fsdp", None),
        P("fsdp", "sp", None),
        P("fsdp", None),
        P("fsdp"),
        P("fsdp", None),
        P("fsdp"),
        P("fsdp"),
        P("fsdp", None),
        P("fsdp"),
        P("fsdp", None),
        P("fsdp"),
        P("fsdp", None),
        P("fsdp"),
    )
    out_specs = (
        P("fsdp", "sp", None),
        P("fsdp", "sp", None),
        P("fsdp", None),
        P(("fsdp", "sp"), None),
        P(("fsdp", "sp")),
        P(("fsdp", "sp"), None),
        P(("fsdp", "sp")),
        P(("fsdp", "sp")),
        P(("fsdp", "sp"), None),
        P(("fsdp", "sp")),
        P(("fsdp", "sp"), None),
        P(("fsdp", "sp")),
        P(("fsdp", "sp"), None),
        P(("fsdp", "sp")),
    )
    return jax.shard_map(body, mesh=mesh, in_specs=in_specs, out_specs=out_specs, check_vma=False)
```
